256 devices in a mesh: wide: 32 (over z, y), narrow: 8 (over x, core).
Axes of the slice: x: 4, y: 4, z: 8, core: 2. Of those that a mesh axis runs over, the one named last changes fastest.
Arguments:
- blocks: float32 [8192, 8, 64, 64], P(('wide', 'narrow'))
- col_index: int32 [8192, 8], P(('wide', 'narrow')), may hold values from 0 to 8191, as said below
- right_side: float32 [16, 524288], P(None, ('wide', 'narrow')), may hold values from -6 to 6
- start_guess: float32 [16, 524288], P(None, ('wide', 'narrow')), may hold values from -3 to 3
Outputs:
- new_guess: float32 [16, 524288], P(None, ('wide', 'narrow'))
- new_residual: float32 [16, 524288], P(None, ('wide', 'narrow'))
The draws below stay inside these ranges and needn't reach their ends.
Inputs may be any that keep to these rules, and one draw needn't show every extreme that they name: col_index[g, 0] = g; the other entries of row g are distinct and differ from g, each at most 8 block rows away from g counted circularly over 8192 block rows.
All inputs are finite; a program needn't handle non-finite values.
Results may differ from the reference program's by a relative error of at most 0.0003.
Values sent between devices are 32-bit elements; how exact they have to be, the bound alone decides.
A program may use at most 64 MiB of HBM per device.

```python
import jax
import jax.numpy as jnp
from jax import lax

BS = 64
NNZB = 8
NRHS = 16
S = 4
BAND = 8
NB = 8192
N = 524288


def draw_col_index(key, part):
    width = 2 * BAND
    offsets = jnp.concatenate([jnp.arange(-BAND, 0), jnp.arange(1, BAND + 1)]).astype(jnp.int32)
    scores = jax.random.randint(key, (NB, width), 0, 1 << 20) * width + jnp.arange(width)[None, :]
    order = jnp.argsort(scores, axis=1, stable=True)[:, :NNZB - 1]
    chosen = offsets[order]
    rows_idx = jnp.arange(NB, dtype=jnp.int32)[:, None]
    others = (rows_idx + chosen + NB) % NB
    return jnp.concatenate([rows_idx, others], axis=1).astype(jnp.int32)


def draw_blocks(key, part):
    first_key, second_key = jax.random.split(key)
    sigma = 0.3 / (NNZB * BS) ** 0.5
    noise = jax.random.normal(first_key, (NB, NNZB, BS, BS), jnp.float32) * sigma
    diag_vals = jax.random.uniform(second_key, (NB, BS), jnp.float32, 1.2, 2.8)
    identity = jnp.eye(BS, dtype=jnp.float32)
    first_block = (jnp.arange(NNZB) == 0).astype(jnp.float32)
    diag_part = first_block[None, :, None, None] * identity[None, None] * diag_vals[:, None, :, None]
    return (noise + diag_part).astype(jnp.float32)


def shard_levels(key, extent, shards, least, high):
    factor_of, own = 1.0, jax.random.fold_in(key, 6)
    for axis_at, blocks in shards:
        steps = jnp.exp(jax.random.uniform(jax.random.fold_in(own, axis_at), (blocks,), jnp.float32, least / len(shards), high / len(shards)))
        factor_of = factor_of * jnp.repeat(steps, extent[axis_at] // blocks).reshape([-1 if axis == axis_at else 1 for axis in range(len(extent))])
    return factor_of


def bell_draw(own_key, shape, spread, most, cuts=(), kind=jnp.bfloat16):
    values = spread * jax.random.normal(own_key, shape, jnp.float32)
    if cuts:
        values = values * shard_levels(own_key, shape, cuts, -0.22, 0.18)
    return jnp.clip(values, -most, most).astype(kind)


def setup_inputs(seed: int = 0) -> dict:
    streams_of = jax.random.split(jax.random.key(seed), 5)
    return {
        "blocks": draw_blocks(jax.random.fold_in(streams_of[4], 71), 0),
        "col_index": draw_col_index(jax.random.fold_in(streams_of[4], 71), 0),
        "right_side": bell_draw(streams_of[2], (NRHS, N), 1.0, 6.0, ((1, 256),), jnp.float32),
        "start_guess": bell_draw(streams_of[3], (NRHS, N), 0.5, 3.0, ((1, 256),), jnp.float32),
    }


def apply_matrix(vec, blocks, col_index):
    nrhs = vec.shape[0]
    shaped = vec.reshape(nrhs, NB, BS)
    total = jnp.zeros((nrhs, NB, BS), jnp.float32)
    for k in range(NNZB):
        picked = jnp.take(shaped, col_index[:, k], axis=1)
        total = total + jnp.einsum('igb,gab->iga', picked, blocks[:, k], precision=lax.Precision.HIGHEST)
    return total.reshape(nrhs, NB * BS)

def reference(blocks, col_index, right_side, start_guess):
    hp = lax.Precision.HIGHEST
    residual = right_side - apply_matrix(start_guess, blocks, col_index)
    vectors = [residual]
    for j in range(S - 1):
        vectors.append(apply_matrix(vectors[-1], blocks, col_index) - 2.0 * vectors[-1])
    basis = jnp.concatenate(vectors, axis=0)
    gram = jnp.dot(basis, basis.T, precision=hp)
    upper = jnp.linalg.cholesky(gram).T
    lower_cols = (S - 1) * NRHS
    hess = upper[:, NRHS:] + 2.0 * upper[:, :lower_cols]
    normal = jnp.dot(hess.T, hess, precision=hp)
    target = jnp.dot(hess.T, upper[:, :NRHS], precision=hp)
    factor = jnp.linalg.cholesky(normal)
    middle = lax.linalg.triangular_solve(factor, target, left_side=True, lower=True)
    coeff = lax.linalg.triangular_solve(factor, middle, left_side=True, lower=True, transpose_a=True)
    low_part = basis[:lower_cols]
    high_part = basis[NRHS:] + 2.0 * low_part
    new_guess = start_guess + jnp.dot(coeff.T, low_part, precision=hp)
    new_residual = residual - jnp.dot(coeff.T, high_part, precision=hp)
    return (new_guess, new_residual)
```

```python
import functools

import jax
import jax.numpy as jnp
from jax import lax
from jax.experimental import pallas as pl
from jax.experimental.pallas import tpu as pltpu
from jax.sharding import Mesh
from jax.sharding import PartitionSpec as P

BS = 64
NNZB = 8
NRHS = 16
S = 4
BAND = 8
ROWS = 32
PAIRS = ROWS // 2
EDGE = BAND // 2
CHUNK = 4
AXES = ("z", "y", "x", "c")
F32 = jnp.float32
BF16 = jnp.bfloat16


def split(v):
    high = v.astype(BF16)
    low = (v - high.astype(F32)).astype(BF16)
    return high, low


def dot_nt(a, b):
    return lax.dot_general(a, b, (((1,), (1,)), ((), ())), preferred_element_type=F32)


def kernel(sizes, col_ref, blocks_hbm, b_hbm, x_hbm, guess_hbm, resid_hbm,
           at_ref, raw, mat, b_ref, x_ref, vec, dup, basis, halves, halo, gram_out, gram_in,
           guess, resid, raw_sem, in_sem, halo0_send, halo0_recv, halo_send, halo_recv,
           red_send, red_recv, out_sem):
    nz, ny, nx, nc = sizes
    total = nz * ny * nx * nc
    here = tuple(lax.axis_index(a) for a in AXES)
    z, y, x, c = here
    linear = ((z * ny + y) * nx + x) * nc + c

    def place(d):
        return (d // (ny * nx * nc), (d // (nx * nc)) % ny, (d // nc) % nx, d % nc)

    up = place((linear + 1) % total)
    down = place((linear + total - 1) % total)

    def narrow_peer(o):
        d = (x * nc + c + o) % (nx * nc)
        return (z, y, d // nc, d % nc)

    def y_peer(o):
        return (z, (y + o) % ny, x, c)

    def z_peer(o):
        return ((z + o) % nz, y, x, c)

    phases = ((nx * nc, narrow_peer), (ny, y_peer), (nz, z_peer))

    def to_remote(src, dst, send, recv, dev):
        return pltpu.make_async_remote_copy(
            src_ref=src, dst_ref=dst, send_sem=send, recv_sem=recv,
            device_id=dev, device_id_type=pl.DeviceIdType.MESH)

    barrier = pltpu.get_barrier_semaphore()
    count = 2
    for dev in (up, down):
        pl.semaphore_signal(barrier, inc=1, device_id=dev, device_id_type=pl.DeviceIdType.MESH)
    for n, peer in phases:
        for o in range(1, n):
            count += 1
            pl.semaphore_signal(barrier, inc=1, device_id=peer(o),
                                device_id_type=pl.DeviceIdType.MESH)

    load_x = pltpu.make_async_copy(x_hbm, x_ref, in_sem.at[0])
    load_b = pltpu.make_async_copy(b_hbm, b_ref, in_sem.at[1])
    load_x.start()
    load_b.start()

    def load_blocks(n):
        rows = pl.ds(n * CHUNK, CHUNK)
        return pltpu.make_async_copy(blocks_hbm.at[rows], raw.at[rows], raw_sem.at[n])

    for n in range(ROWS // CHUNK):
        load_blocks(n).start()
    first_row = linear * ROWS

    def locate(g, _):
        for k in range(NNZB):
            at = jnp.bitwise_and(col_ref[k, g] - first_row + BAND + total * ROWS,
                                 total * ROWS - 1)
            at_ref[k, g] = jnp.minimum(at, ROWS + 2 * BAND - 1)
        return 0

    lax.fori_loop(0, ROWS, locate, 0)
    pl.semaphore_wait(barrier, count)

    def first_halo(side, q):
        tile = q if side == 1 else PAIRS - EDGE + q
        return to_remote(x_hbm.at[:, pl.ds(tile * 128, 128)], halo.at[0, side, q],
                         halo0_send.at[side, q], halo0_recv.at[side, q],
                         down if side == 1 else up)

    def later_halo(j, side):
        start = 0 if side == 1 else PAIRS - EDGE
        return to_remote(basis.at[j - 1, pl.ds(start, EDGE)], halo.at[j, side],
                         halo_send.at[j - 1, side], halo_recv.at[j - 1, side],
                         down if side == 1 else up)

    for q in range(EDGE):
        for side in range(2):
            first_halo(side, q).start()

    left = lax.broadcasted_iota(jnp.int32, (NRHS, 128), 1) < BS
    left2 = lax.broadcasted_iota(jnp.int32, (2 * NRHS, 128), 1) < BS

    def both(v):
        r = pltpu.roll(v, BS, 1)
        return jnp.where(left, v, r), jnp.where(left, r, v)

    def put(j, row, v):
        high, low = split(v)
        vec[j, row, 0:NRHS] = high
        vec[j, row, NRHS:2 * NRHS] = low

    load_x.wait()
    load_b.wait()

    def spread(p, _):
        lanes = pl.ds(pl.multiple_of(p * 128, 128), 128)
        v0, v1 = both(-x_ref[:, lanes])
        put(0, BAND + 2 * p, v0)
        put(0, BAND + 2 * p + 1, v1)
        w0, w1 = both(b_ref[:, lanes])
        dup[2 * p] = w0
        dup[2 * p + 1] = w1
        return 0

    lax.fori_loop(0, PAIRS, spread, 0)

    def prepare_row(g):
        for m in range(NNZB // 2):
            wide = jnp.concatenate([raw[g, 2 * m], raw[g, 2 * m + 1]], axis=1)
            high, low = split(wide)
            mat[g, 0:BS, m * 128:(m + 1) * 128] = high
            mat[g, BS:2 * BS, m * 128:(m + 1) * 128] = low

    def prepare(n, _):
        load_blocks(n).wait()
        for r in range(CHUNK):
            prepare_row(n * CHUNK + r)
        return 0

    lax.fori_loop(0, ROWS // CHUNK, prepare, 0)

    def apply_row(j, g, beta):
        tiles = []
        for m in range(NNZB // 2):
            part = []
            for k in (2 * m, 2 * m + 1):
                part.append(vec[j, at_ref[k, g]])
            tiles.append(jnp.where(left2, part[0], part[1]))
        out = dot_nt(jnp.concatenate(tiles, axis=1), mat[g])
        half = out[0:NRHS] + out[NRHS:2 * NRHS]
        v = half + pltpu.roll(half, BS, 1) + beta * dup[g]
        dup[g] = v
        put(j + 1, BAND + g, v)
        return v

    def apply_pair(j, p, beta):
        v0 = apply_row(j, 2 * p, beta)
        v1 = apply_row(j, 2 * p + 1, beta)
        v = jnp.where(left, v0, v1)
        basis[j, p] = v
        high, low = split(v)
        halves[p, 0, j] = high
        halves[p, 1, j] = low

    def apply_pairs(j, start, n, beta):
        def body(i, _):
            for t in range(4):
                apply_pair(j, start + i * 4 + t, beta)
            return 0
        lax.fori_loop(0, n // 4, body, 0)

    def take_halo(j, side, sign):
        for q in range(EDGE):
            v0, v1 = both(sign * halo[j, side, q])
            row = 2 * q + (0 if side == 0 else BAND + ROWS)
            put(j, row, v0)
            put(j, row + 1, v1)

    def step(j, _):
        beta = jnp.where(j == 0, 1.0, -2.0)
        sign = jnp.where(j == 0, -1.0, 1.0)
        apply_pairs(j, EDGE, PAIRS - 2 * EDGE, beta)

        @pl.when(j == 0)
        def _():
            for side in range(2):
                for q in range(EDGE):
                    first_halo(side, q).wait_recv()

        @pl.when(j > 0)
        def _():
            for side in range(2):
                later_halo(j, side).wait_recv()

        take_halo(j, 0, sign)
        take_halo(j, 1, sign)
        for side in (1, 0):
            start = 0 if side == 1 else PAIRS - EDGE
            apply_pairs(j, start, EDGE, beta)

            @pl.when(j < S - 1)
            def _():
                later_halo(j + 1, side).start()
        return 0

    lax.fori_loop(0, S, step, 0)

    gram = jnp.zeros((2 * S * NRHS, 128), F32)
    for p in range(0, PAIRS, 2):
        tile = jnp.concatenate([halves[p].reshape(2 * S * NRHS, 128),
                                halves[p + 1].reshape(2 * S * NRHS, 128)], axis=1)
        gram = gram + dot_nt(tile, tile)
    gram = gram[0:64] + gram[64:128]
    gram = gram + pltpu.roll(gram, 64, 1)
    left3 = lax.broadcasted_iota(jnp.int32, (32, 128), 1) < 64
    packed = jnp.where(left3, gram[0:32], gram[32:64])

    sent = []
    base = 0
    for f, (n, peer) in enumerate(phases):
        gram_out[f] = packed
        copies = []
        for o in range(1, n):
            copy = to_remote(gram_out.at[f], gram_in.at[base + o - 1],
                             red_send.at[base + o - 1], red_recv.at[base + o - 1], peer(o))
            copy.start()
            copies.append(copy)
        for o in range(1, n):
            copies[o - 1].wait_recv()
            packed = packed + gram_in[base + o - 1]
        sent += copies
        base += n - 1

    turned = pltpu.roll(packed, 64, 1)
    gram = jnp.concatenate([jnp.where(left3, packed, turned),
                            jnp.where(left3, turned, packed)], axis=0)

    lane = lax.broadcasted_iota(jnp.int32, (48, 128), 1)
    sub = lax.broadcasted_iota(jnp.int32, (48, 128), 0)
    hess = gram[16:64] + 2.0 * gram[0:48]
    system = pltpu.roll(hess, 112, 1) + jnp.where(lane % 64 < 48, 2.0 * hess, 0.0)
    for k in range(48):
        row = jnp.broadcast_to(system[k:k + 1, :], (48, 128))
        col = jnp.broadcast_to(system[:, k:k + 1], (48, 128))
        scaled = row * (1.0 / jnp.broadcast_to(system[k:k + 1, k:k + 1], (1, 128)))
        system = jnp.where(sub == k, scaled, system - col * scaled)

    none = jnp.zeros((16, 128), F32)
    low_coeff = jnp.concatenate([system, none], axis=0)
    high_coeff = jnp.concatenate([none, system], axis=0) + 2.0 * low_coeff
    lane = lax.broadcasted_iota(jnp.int32, (64, 128), 1)
    mix = jnp.where(lane < 16, pltpu.roll(low_coeff, 80, 1), pltpu.roll(-high_coeff, 96, 1))
    mix = jnp.transpose(mix)[0:32]

    outs = []
    for p in range(0, PAIRS, 4):
        tile = jnp.concatenate([basis[:, p + t].reshape(64, 128) for t in range(4)], axis=1)
        out = jnp.dot(mix, tile, precision=lax.Precision.HIGHEST, preferred_element_type=F32)
        lanes = slice(p * 128, (p + 4) * 128)
        guess[:, lanes] = x_ref[:, lanes] + out[0:16]
        resid[:, lanes] = tile[0:16] + out[16:32]
        for w, (src, dst) in enumerate(((guess, guess_hbm), (resid, resid_hbm))):
            copy = pltpu.make_async_copy(src.at[:, lanes], dst.at[:, lanes],
                                         out_sem.at[w, p // 4])
            copy.start()
            outs.append(copy)

    for side in range(2):
        for q in range(EDGE):
            first_halo(side, q).wait_send()
        for j in range(1, S):
            later_halo(j, side).wait_send()
    for copy in sent:
        copy.wait_send()
    for copy in outs:
        copy.wait()


def per_device(sizes, blocks, col_index, right_side, start_guess):
    n_red = sizes[0] - 1 + sizes[1] - 1 + sizes[2] * sizes[3] - 1
    anywhere = pl.BlockSpec(memory_space=pltpu.HBM)
    dma = pltpu.SemaphoreType.DMA
    out = jax.ShapeDtypeStruct((NRHS, ROWS * BS), F32)
    return pl.pallas_call(
        functools.partial(kernel, sizes),
        out_shape=(out, out),
        in_specs=[pl.BlockSpec(memory_space=pltpu.SMEM), anywhere, anywhere, anywhere],
        out_specs=(anywhere, anywhere),
        scratch_shapes=[
            pltpu.SMEM((NNZB, ROWS), jnp.int32),
            pltpu.VMEM((ROWS, NNZB, BS, BS), F32),
            pltpu.VMEM((ROWS, 2 * BS, NNZB * BS), BF16),
            pltpu.VMEM((NRHS, ROWS * BS), F32),
            pltpu.VMEM((NRHS, ROWS * BS), F32),
            pltpu.VMEM((S + 1, ROWS + 2 * BAND, 2 * NRHS, 128), BF16),
            pltpu.VMEM((ROWS, NRHS, 128), F32),
            pltpu.VMEM((S, PAIRS, NRHS, 128), F32),
            pltpu.VMEM((PAIRS, 2, S, NRHS, 128), BF16),
            pltpu.VMEM((S, 2, EDGE, NRHS, 128), F32),
            pltpu.VMEM((3, 32, 128), F32),
            pltpu.VMEM((n_red, 32, 128), F32),
            pltpu.VMEM((NRHS, ROWS * BS), F32),
            pltpu.VMEM((NRHS, ROWS * BS), F32),
            dma((ROWS // CHUNK,)),
            dma((2,)),
            dma((2, EDGE)),
            dma((2, EDGE)),
            dma((S - 1, 2)),
            dma((S - 1, 2)),
            dma((n_red,)),
            dma((n_red,)),
            dma((2, PAIRS // 4)),
        ],
        compiler_params=pltpu.CompilerParams(
            collective_id=0, has_side_effects=True, vmem_limit_bytes=48 * 1024 * 1024),
        name="gmres_cycle",
    )(col_index.T, blocks, right_side, start_guess)


def solution(mesh, sizes=(8, 4, 4, 2)):
    torus = Mesh(mesh.devices.reshape(sizes), AXES)
    in_specs = (P(AXES, None, None, None), P(AXES, None), P(None, AXES), P(None, AXES))
    out_specs = (P(None, AXES), P(None, AXES))
    return jax.shard_map(functools.partial(per_device, sizes), mesh=torus, in_specs=in_specs,
                         out_specs=out_specs, check_vma=False)
```

```python
import functools

import jax
import jax.numpy as jnp
from jax import lax
from jax.experimental import pallas as pl
from jax.experimental.pallas import tpu as pltpu
from jax.sharding import Mesh
from jax.sharding import PartitionSpec as P

BS = 64
NNZB = 8
NRHS = 16
S = 4
BAND = 8
ROWS = 32
PAIRS = ROWS // 2
EDGE = BAND // 2
CHUNK = 4
AXES = ("z", "y", "x", "c")
F32 = jnp.float32
BF16 = jnp.bfloat16


def split(v):
    high = v.astype(BF16)
    low = (v - high.astype(F32)).astype(BF16)
    return high, low


def dot_nt(a, b):
    return lax.dot_general(a, b, (((1,), (1,)), ((), ())), preferred_element_type=F32)


def eliminate(system, start, n):
    rows = system.shape[0]
    sub = lax.broadcasted_iota(jnp.int32, system.shape, 0)
    for k in range(start, start + n):
        row = jnp.broadcast_to(system[k:k + 1, :], system.shape)
        col = jnp.broadcast_to(system[:, k:k + 1], system.shape)
        scaled = row * (1.0 / jnp.broadcast_to(system[k:k + 1, k:k + 1], (1, 128)))
        system = jnp.where(sub == k, scaled, system - col * scaled)
    return system


def kernel(sizes, col_ref, blocks_hbm, b_hbm, x_hbm, guess_hbm, resid_hbm,
           at_ref, raw, mat, b_ref, x_ref, vec, dup, basis, halves, halo, early_out, early_in, late_out, late_in,
           guess, resid, raw_sem, in_sem, halo0_send, halo0_recv, halo_send, halo_recv,
           red_send, red_recv, out_sem):
    nz, ny, nx, nc = sizes
    total = nz * ny * nx * nc
    here = tuple(lax.axis_index(a) for a in AXES)
    z, y, x, c = here
    linear = ((z * ny + y) * nx + x) * nc + c

    def place(d):
        return (d // (ny * nx * nc), (d // (nx * nc)) % ny, (d // nc) % nx, d % nc)

    up = place((linear + 1) % total)
    down = place((linear + total - 1) % total)

    def plane_peer(o):
        d = ((y * nx + x) * nc + c + o) % (ny * nx * nc)
        return (z, d // (nx * nc), (d // nc) % nx, d % nc)

    def z_peer(o):
        return ((z + o) % nz, y, x, c)

    phases = ((ny * nx * nc, plane_peer), (nz, z_peer))

    def to_remote(src, dst, send, recv, dev):
        return pltpu.make_async_remote_copy(
            src_ref=src, dst_ref=dst, send_sem=send, recv_sem=recv,
            device_id=dev, device_id_type=pl.DeviceIdType.MESH)

    barrier = pltpu.get_barrier_semaphore()
    count = 2
    for dev in (up, down):
        pl.semaphore_signal(barrier, inc=1, device_id=dev, device_id_type=pl.DeviceIdType.MESH)
    for n, peer in phases:
        for o in range(1, n):
            count += 1
            pl.semaphore_signal(barrier, inc=1, device_id=peer(o),
                                device_id_type=pl.DeviceIdType.MESH)

    load_x = pltpu.make_async_copy(x_hbm, x_ref, in_sem.at[0])
    load_b = pltpu.make_async_copy(b_hbm, b_ref, in_sem.at[1])
    load_x.start()
    load_b.start()

    def load_blocks(n):
        rows = pl.ds(n * CHUNK, CHUNK)
        return pltpu.make_async_copy(blocks_hbm.at[rows], raw.at[rows], raw_sem.at[n])

    for n in range(ROWS // CHUNK):
        load_blocks(n).start()
    first_row = linear * ROWS

    def locate(g, _):
        for k in range(NNZB):
            at = jnp.bitwise_and(col_ref[k, g] - first_row + BAND + total * ROWS,
                                 total * ROWS - 1)
            at_ref[k, g] = jnp.minimum(at, ROWS + 2 * BAND - 1)
        return 0

    lax.fori_loop(0, ROWS, locate, 0)
    pl.semaphore_wait(barrier, count)

    def first_halo(side, q):
        tile = q if side == 1 else PAIRS - EDGE + q
        return to_remote(x_hbm.at[:, pl.ds(tile * 128, 128)], halo.at[0, side, q],
                         halo0_send.at[side, q], halo0_recv.at[side, q],
                         down if side == 1 else up)

    def later_halo(j, side):
        start = 0 if side == 1 else PAIRS - EDGE
        return to_remote(basis.at[j - 1, pl.ds(start, EDGE)], halo.at[j, side],
                         halo_send.at[j - 1, side], halo_recv.at[j - 1, side],
                         down if side == 1 else up)

    for q in range(EDGE):
        for side in range(2):
            first_halo(side, q).start()

    left = lax.broadcasted_iota(jnp.int32, (NRHS, 128), 1) < BS
    left2 = lax.broadcasted_iota(jnp.int32, (2 * NRHS, 128), 1) < BS

    def both(v):
        r = pltpu.roll(v, BS, 1)
        return jnp.where(left, v, r), jnp.where(left, r, v)

    def put(j, row, v):
        high, low = split(v)
        vec[j, row, 0:NRHS] = high
        vec[j, row, NRHS:2 * NRHS] = low

    load_x.wait()
    load_b.wait()

    def spread(p, _):
        lanes = pl.ds(pl.multiple_of(p * 128, 128), 128)
        v0, v1 = both(-x_ref[:, lanes])
        put(0, BAND + 2 * p, v0)
        put(0, BAND + 2 * p + 1, v1)
        w0, w1 = both(b_ref[:, lanes])
        dup[2 * p] = w0
        dup[2 * p + 1] = w1
        return 0

    lax.fori_loop(0, PAIRS, spread, 0)

    def prepare_row(g):
        for m in range(NNZB // 2):
            wide = jnp.concatenate([raw[g, 2 * m], raw[g, 2 * m + 1]], axis=1)
            high, low = split(wide)
            mat[g, 0:BS, m * 128:(m + 1) * 128] = high
            mat[g, BS:2 * BS, m * 128:(m + 1) * 128] = low

    def prepare(n, _):
        load_blocks(n).wait()
        for r in range(CHUNK):
            prepare_row(n * CHUNK + r)
        return 0

    lax.fori_loop(0, ROWS // CHUNK, prepare, 0)

    def apply_pairs(j, pairs, beta):
        halfs = []
        for p in pairs:
            for g in (2 * p, 2 * p + 1):
                tiles = []
                for m in range(NNZB // 2):
                    tiles.append(jnp.where(left2, vec[j, at_ref[2 * m, g]],
                                           vec[j, at_ref[2 * m + 1, g]]))
                out = dot_nt(jnp.concatenate(tiles, axis=1), mat[g])
                halfs.append(out[0:NRHS] + out[NRHS:2 * NRHS])
        for i, p in enumerate(pairs):
            v = []
            for g in (0, 1):
                half = halfs[2 * i + g]
                v.append(half + pltpu.roll(half, BS, 1) + beta * dup[2 * p + g])
            for g in (0, 1):
                dup[2 * p + g] = v[g]
                put(j + 1, BAND + 2 * p + g, v[g])
            both_rows = jnp.where(left, v[0], v[1])
            basis[j, p] = both_rows
            high, low = split(both_rows)
            halves[p, 0, j] = high
            halves[p, 1, j] = low

    def take_halo(j, side, sign):
        for q in range(EDGE):
            v0, v1 = both(sign * halo[j, side, q])
            row = 2 * q + (0 if side == 0 else BAND + ROWS)
            put(j, row, v0)
            put(j, row + 1, v1)

    def wait_first():
        for side in range(2):
            for q in range(EDGE):
                first_halo(side, q).wait_recv()

    def wait_later(j):
        for side in range(2):
            later_halo(j, side).wait_recv()

    def edges(j, beta, sign, last):
        take_halo(j, 0, sign)
        take_halo(j, 1, sign)
        for side in (1, 0):
            start = 0 if side == 1 else PAIRS - EDGE
            apply_pairs(j, range(start, start + EDGE), beta)
            if not last:
                later_halo(j + 1, side).start()

    def step(j, _):
        beta = jnp.where(j == 0, 1.0, -2.0)
        sign = jnp.where(j == 0, -1.0, 1.0)
        apply_pairs(j, range(EDGE, PAIRS - EDGE), beta)

        @pl.when(j == 0)
        def _():
            wait_first()

        @pl.when(j > 0)
        def _():
            wait_later(j)

        edges(j, beta, sign, False)
        return 0

    def products(rows, cols, start, n):
        total_products = None
        for p in range(start, start + n, 2):
            def tile(js):
                return jnp.concatenate(
                    [halves[q][:, js].reshape(2 * len(range(S)[js]) * NRHS, 128)
                     for q in (p, p + 1)], axis=1)
            part = dot_nt(tile(rows), tile(cols))
            total_products = part if total_products is None else total_products + part
        return total_products

    def fold(g):
        n = g.shape[0] // 2
        g = g[0:n] + g[n:2 * n]
        return g + pltpu.roll(g, 64, 1)

    def pack(g):
        n = g.shape[0] // 2
        mask = lax.broadcasted_iota(jnp.int32, (n, 128), 1) < 64
        return jnp.where(mask, g[0:n], g[n:2 * n])

    def unpack(g):
        n = g.shape[0]
        mask = lax.broadcasted_iota(jnp.int32, (n, 128), 1) < 64
        r = pltpu.roll(g, 64, 1)
        return jnp.concatenate([jnp.where(mask, g, r), jnp.where(mask, r, g)], axis=0)

    spans = []
    base = 0
    for n, _ in phases:
        spans.append((base, n))
        base += n - 1

    def sum_copies(r, f):
        out, inn = (early_out, early_in) if r == 0 else (late_out, late_in)
        base, n = spans[f]
        return [to_remote(out.at[f], inn.at[base + o - 1], red_send.at[r, base + o - 1],
                          red_recv.at[r, base + o - 1], phases[f][1](o)) for o in range(1, n)]

    def sum_start(r, f, value):
        (early_out if r == 0 else late_out)[f] = value
        for copy in sum_copies(r, f):
            copy.start()

    def sum_finish(r, f, value):
        inn = early_in if r == 0 else late_in
        base, n = spans[f]
        for o, copy in enumerate(sum_copies(r, f)):
            copy.wait_recv()
        parts = [value] + [inn[base + o] for o in range(n - 1)]
        while len(parts) > 1:
            parts = [parts[i] + parts[i + 1] if i + 1 < len(parts) else parts[i]
                     for i in range(0, len(parts), 2)]
        return parts[0]

    lax.fori_loop(0, S - 1, step, 0)
    halves[:, :, S - 1] = jnp.zeros((PAIRS, 2, NRHS, 128), BF16)
    gram = products(slice(0, 3), slice(0, 4), 0, PAIRS)
    early = pack(fold(gram))
    sum_start(0, 0, early)
    apply_pairs(S - 1, range(EDGE, PAIRS - EDGE), -2.0)
    wait_later(S - 1)
    edges(S - 1, -2.0, 1.0, True)
    late = pack(fold(products(slice(3, 4), slice(0, 4), 0, PAIRS)))
    sum_start(1, 0, late)
    early = sum_finish(0, 0, early)
    sum_start(0, 1, early)
    late = sum_finish(1, 0, late)
    sum_start(1, 1, late)
    early = sum_finish(0, 1, early)

    gram = unpack(early)
    lane32 = lax.broadcasted_iota(jnp.int32, (32, 128), 1)
    sub32 = lax.broadcasted_iota(jnp.int32, (32, 128), 0)
    hess = gram[16:48] + 2.0 * gram[0:32]
    system = pltpu.roll(hess, 112, 1) + jnp.where(lane32 % 64 < 48, 2.0 * hess, 0.0)
    system = jnp.where(lane32 < 64, system, jnp.where(lane32 - 64 == sub32, 1.0, 0.0))
    system = eliminate(system, 0, 32)

    late = unpack(sum_finish(1, 1, late))
    lane16 = lax.broadcasted_iota(jnp.int32, (16, 128), 1)
    turned = jnp.transpose(jnp.concatenate([late, jnp.zeros((112, 128), F32)], axis=0))
    row2 = jnp.where(lane16 % 64 < 48, gram[32:48],
                     pltpu.roll(turned[32:48], 48, 1))
    hess2 = late + 2.0 * row2
    cross = pltpu.roll(hess2, 112, 1) + jnp.where(lane16 % 64 < 48, 2.0 * hess2, 0.0)
    hp = lax.Precision.HIGHEST
    moved = jnp.dot(cross[:, 0:32], system, precision=hp, preferred_element_type=F32)
    inner = lax.dot_general(moved[:, 64:96], cross[:, 0:32], (((1,), (1,)), ((), ())),
                            precision=hp, preferred_element_type=F32)
    inner = jnp.concatenate([inner, jnp.zeros((16, 112), F32)], axis=1)
    schur = jnp.where(lane16 < 16, pltpu.roll(cross, 96, 1) - inner,
                      pltpu.roll(cross - moved, 96, 1))
    schur = eliminate(schur, 0, 16)
    last = pltpu.roll(schur, 32, 1)
    back = jnp.transpose(jnp.concatenate([moved, jnp.zeros((112, 128), F32)], axis=0))[64:96, 0:16]
    first = system - jnp.dot(back, last, precision=hp, preferred_element_type=F32)
    system = jnp.concatenate([first, last], axis=0)

    none = jnp.zeros((16, 128), F32)
    low_coeff = jnp.concatenate([system, none], axis=0)
    high_coeff = jnp.concatenate([none, system], axis=0) + 2.0 * low_coeff
    lane = lax.broadcasted_iota(jnp.int32, (64, 128), 1)
    mix = jnp.where(lane < 16, pltpu.roll(low_coeff, 80, 1), pltpu.roll(-high_coeff, 96, 1))
    mix = jnp.transpose(mix)[0:32]

    outs = []
    for p in range(0, PAIRS, 4):
        tile = jnp.concatenate([basis[:, p + t].reshape(64, 128) for t in range(4)], axis=1)
        out = jnp.dot(mix, tile, precision=lax.Precision.HIGHEST, preferred_element_type=F32)
        lanes = slice(p * 128, (p + 4) * 128)
        guess[:, lanes] = x_ref[:, lanes] + out[0:16]
        resid[:, lanes] = tile[0:16] + out[16:32]
        for w, (src, dst) in enumerate(((guess, guess_hbm), (resid, resid_hbm))):
            copy = pltpu.make_async_copy(src.at[:, lanes], dst.at[:, lanes],
                                         out_sem.at[w, p // 4])
            copy.start()
            outs.append(copy)

    for side in range(2):
        for q in range(EDGE):
            first_halo(side, q).wait_send()
        for j in range(1, S):
            later_halo(j, side).wait_send()
    for r in range(2):
        for f in range(2):
            for copy in sum_copies(r, f):
                copy.wait_send()
    for copy in outs:
        copy.wait()


def per_device(sizes, blocks, col_index, right_side, start_guess):
    n_red = sizes[0] - 1 + sizes[1] * sizes[2] * sizes[3] - 1
    anywhere = pl.BlockSpec(memory_space=pltpu.HBM)
    dma = pltpu.SemaphoreType.DMA
    out = jax.ShapeDtypeStruct((NRHS, ROWS * BS), F32)
    return pl.pallas_call(
        functools.partial(kernel, sizes),
        out_shape=(out, out),
        in_specs=[pl.BlockSpec(memory_space=pltpu.SMEM), anywhere, anywhere, anywhere],
        out_specs=(anywhere, anywhere),
        scratch_shapes=[
            pltpu.SMEM((NNZB, ROWS), jnp.int32),
            pltpu.VMEM((ROWS, NNZB, BS, BS), F32),
            pltpu.VMEM((ROWS, 2 * BS, NNZB * BS), BF16),
            pltpu.VMEM((NRHS, ROWS * BS), F32),
            pltpu.VMEM((NRHS, ROWS * BS), F32),
            pltpu.VMEM((S + 1, ROWS + 2 * BAND, 2 * NRHS, 128), BF16),
            pltpu.VMEM((ROWS, NRHS, 128), F32),
            pltpu.VMEM((S, PAIRS, NRHS, 128), F32),
            pltpu.VMEM((PAIRS, 2, S, NRHS, 128), BF16),
            pltpu.VMEM((S, 2, EDGE, NRHS, 128), F32),
            pltpu.VMEM((2, 24, 128), F32),
            pltpu.VMEM((n_red, 24, 128), F32),
            pltpu.VMEM((2, 8, 128), F32),
            pltpu.VMEM((n_red, 8, 128), F32),
            pltpu.VMEM((NRHS, ROWS * BS), F32),
            pltpu.VMEM((NRHS, ROWS * BS), F32),
            dma((ROWS // CHUNK,)),
            dma((2,)),
            dma((2, EDGE)),
            dma((2, EDGE)),
            dma((S - 1, 2)),
            dma((S - 1, 2)),
            dma((2, n_red)),
            dma((2, n_red)),
            dma((2, PAIRS // 4)),
        ],
        compiler_params=pltpu.CompilerParams(
            collective_id=0, has_side_effects=True, vmem_limit_bytes=62 * 1024 * 1024),
        name="gmres_cycle",
    )(col_index.T, blocks, right_side, start_guess)


def solution(mesh, sizes=(8, 4, 4, 2)):
    torus = Mesh(mesh.devices.reshape(sizes), AXES)
    in_specs = (P(AXES, None, None, None), P(AXES, None), P(None, AXES), P(None, AXES))
    out_specs = (P(None, AXES), P(None, AXES))
    return jax.shard_map(functools.partial(per_device, sizes), mesh=torus, in_specs=in_specs,
                         out_specs=out_specs, check_vma=False)
```

```python
import functools
import itertools

import jax
import jax.numpy as jnp
from jax import lax
from jax.experimental import pallas as pl
from jax.experimental.pallas import tpu as pltpu
from jax.sharding import Mesh
from jax.sharding import PartitionSpec as P

BS = 64
NNZB = 8
NRHS = 16
S = 4
BAND = 8
ROWS = 32
PAIRS = ROWS // 2
EDGE = BAND // 2
CHUNK = 4
AXES = ("z", "y", "x", "c")
F32 = jnp.float32
BF16 = jnp.bfloat16


def PHASES(sizes):
    nz, ny, nx, nc = sizes
    one = range(1)
    return ((one, range(ny), range(nx), range(nc)), (range(nz), one, one, one))


def split(v):
    high = v.astype(BF16)
    low = (v - high.astype(F32)).astype(BF16)
    return high, low


def dot_nt(a, b):
    return lax.dot_general(a, b, (((1,), (1,)), ((), ())), preferred_element_type=F32)


def eliminate(system, start, n):
    rows = system.shape[0]
    sub = lax.broadcasted_iota(jnp.int32, system.shape, 0)
    for k in range(start, start + n):
        row = jnp.broadcast_to(system[k:k + 1, :], system.shape)
        col = jnp.broadcast_to(system[:, k:k + 1], system.shape)
        scaled = row * (1.0 / jnp.broadcast_to(system[k:k + 1, k:k + 1], (1, 128)))
        system = jnp.where(sub == k, scaled, system - col * scaled)
    return system


def kernel(sizes, col_ref, blocks_hbm, b_hbm, x_hbm, guess_hbm,
           at_ref, raw, mat, b_ref, x_ref, vec, dup, basis, halves, halo, early_out, early_in, late_out, late_in,
           guess, raw_sem, in_sem, halo0_send, halo0_recv, halo_send, halo_recv,
           red_send, red_recv, out_sem):
    nz, ny, nx, nc = sizes
    total = nz * ny * nx * nc
    here = tuple(lax.axis_index(a) for a in AXES)
    z, y, x, c = here
    linear = ((z * ny + y) * nx + x) * nc + c

    def place(d):
        return (d // (ny * nx * nc), (d // (nx * nc)) % ny, (d // nc) % nx, d % nc)

    up = place((linear + 1) % total)
    down = place((linear + total - 1) % total)

    def offsets(zs, ys, xs, cs):
        def hops(d):
            return sum(min(v, n - v) for v, n in zip(d[:3], (nz, ny, nx)))
        found = [d for d in itertools.product(zs, ys, xs, cs) if any(d)]
        return sorted(found, key=lambda d: (-hops(d), d))

    def peer(d):
        return tuple((v + o) % n for v, o, n in zip(here, d, sizes))

    phases = tuple(offsets(*span) for span in PHASES(sizes))
    order = jnp.where(linear % (nx * nc) == nx * nc - 1, 1, 0)

    def to_remote(src, dst, send, recv, dev):
        return pltpu.make_async_remote_copy(
            src_ref=src, dst_ref=dst, send_sem=send, recv_sem=recv,
            device_id=dev, device_id_type=pl.DeviceIdType.MESH)

    barrier = pltpu.get_barrier_semaphore()
    count = 2
    for dev in (up, down):
        pl.semaphore_signal(barrier, inc=1, device_id=dev, device_id_type=pl.DeviceIdType.MESH)
    for d in sorted(phases[0] + phases[1], key=lambda d: -sum(min(v, n - v) for v, n in zip(d, sizes))):
        count += 1
        pl.semaphore_signal(barrier, inc=1, device_id=peer(d),
                            device_id_type=pl.DeviceIdType.MESH)

    load_x = pltpu.make_async_copy(x_hbm, x_ref, in_sem.at[0])
    load_b = pltpu.make_async_copy(b_hbm, b_ref, in_sem.at[1])
    load_x.start()
    load_b.start()

    def load_blocks(n):
        rows = pl.ds(n * CHUNK, CHUNK)
        return pltpu.make_async_copy(blocks_hbm.at[rows], raw.at[rows], raw_sem.at[n])

    for n in range(ROWS // CHUNK):
        load_blocks(n).start()
    first_row = linear * ROWS

    def locate(g, _):
        for k in range(NNZB):
            at = jnp.bitwise_and(col_ref[k, g] - first_row + BAND + total * ROWS,
                                 total * ROWS - 1)
            at_ref[k, g] = jnp.minimum(at, ROWS + 2 * BAND - 1)
        return 0

    lax.fori_loop(0, ROWS, locate, 0)
    pl.semaphore_wait(barrier, count)

    def neighbour(w):
        return tuple(jnp.where(w == 1, u, d) for u, d in zip(up, down))

    def first_halo(w, q):
        tile = q + w * (PAIRS - EDGE)
        return to_remote(x_hbm.at[:, pl.ds(pl.multiple_of(tile * 128, 128), 128)],
                         halo.at[0, 1 - w, q], halo0_send.at[w, q], halo0_recv.at[1 - w, q],
                         neighbour(w))

    def later_halo(j, w):
        return to_remote(basis.at[j - 1, pl.ds(w * (PAIRS - EDGE), EDGE)], halo.at[j, 1 - w],
                         halo_send.at[j - 1, w], halo_recv.at[j - 1, 1 - w], neighbour(w))

    for w in (order, 1 - order):
        for q in range(EDGE):
            first_halo(w, q).start()

    left = lax.broadcasted_iota(jnp.int32, (NRHS, 128), 1) < BS
    left2 = lax.broadcasted_iota(jnp.int32, (2 * NRHS, 128), 1) < BS

    def both(v):
        r = pltpu.roll(v, BS, 1)
        return jnp.where(left, v, r), jnp.where(left, r, v)

    def put(j, row, v):
        high, low = split(v)
        vec[j, row, 0:NRHS] = high
        vec[j, row, NRHS:2 * NRHS] = low

    load_x.wait()
    load_b.wait()

    def spread(p, _):
        lanes = pl.ds(pl.multiple_of(p * 128, 128), 128)
        v0, v1 = both(-x_ref[:, lanes])
        put(0, BAND + 2 * p, v0)
        put(0, BAND + 2 * p + 1, v1)
        w0, w1 = both(b_ref[:, lanes])
        dup[2 * p] = w0
        dup[2 * p + 1] = w1
        return 0

    lax.fori_loop(0, PAIRS, spread, 0)

    def prepare_row(g):
        for m in range(NNZB // 2):
            wide = jnp.concatenate([raw[g, 2 * m], raw[g, 2 * m + 1]], axis=1)
            high, low = split(wide)
            mat[g, 0:BS, m * 128:(m + 1) * 128] = high
            mat[g, BS:2 * BS, m * 128:(m + 1) * 128] = low

    def prepare(n, _):
        load_blocks(n).wait()
        for r in range(CHUNK):
            prepare_row(n * CHUNK + r)
        return 0

    lax.fori_loop(0, ROWS // CHUNK, prepare, 0)

    def apply_pairs(j, pairs, beta):
        halfs = []
        for p in pairs:
            for g in (2 * p, 2 * p + 1):
                tiles = []
                for m in range(NNZB // 2):
                    tiles.append(jnp.where(left2, vec[j, at_ref[2 * m, g]],
                                           vec[j, at_ref[2 * m + 1, g]]))
                out = dot_nt(jnp.concatenate(tiles, axis=1), mat[g])
                halfs.append(out[0:NRHS] + out[NRHS:2 * NRHS])
        for i, p in enumerate(pairs):
            v = []
            for g in (0, 1):
                half = halfs[2 * i + g]
                v.append(half + pltpu.roll(half, BS, 1) + beta * dup[2 * p + g])
            for g in (0, 1):
                dup[2 * p + g] = v[g]
                put(j + 1, BAND + 2 * p + g, v[g])
            both_rows = jnp.where(left, v[0], v[1])
            basis[j, p] = both_rows
            high, low = split(both_rows)
            halves[p, 0, j] = high
            halves[p, 1, j] = low

    def take_halo(j, w, sign):
        for q in range(EDGE):
            v0, v1 = both(sign * halo[j, w, q])
            row = 2 * q + w * (BAND + ROWS)
            put(j, row, v0)
            put(j, row + 1, v1)

    def edges(j, beta, sign, first, last):
        for w in (order, 1 - order):
            if first is None:
                later_halo(j, 1 - w).wait_recv()
            else:
                @pl.when(first)
                def _():
                    for q in range(EDGE):
                        first_halo(1 - w, q).wait_recv()

                @pl.when(jnp.logical_not(first))
                def _():
                    later_halo(j, 1 - w).wait_recv()

            take_halo(j, w, sign)
            start = w * (PAIRS - EDGE)
            apply_pairs(j, [start + i for i in range(EDGE)], beta)
            if not last:
                later_halo(j + 1, w).start()

    def step(j, _):
        beta = jnp.where(j == 0, 1.0, -2.0)
        sign = jnp.where(j == 0, -1.0, 1.0)
        apply_pairs(j, range(EDGE, PAIRS - EDGE), beta)
        edges(j, beta, sign, j == 0, False)
        return 0

    def products(rows, cols, start, n):
        total_products = None
        for p in range(start, start + n, 2):
            def tile(js):
                return jnp.concatenate(
                    [halves[q][:, js].reshape(2 * len(range(S)[js]) * NRHS, 128)
                     for q in (p, p + 1)], axis=1)
            part = dot_nt(tile(rows), tile(cols))
            total_products = part if total_products is None else total_products + part
        return total_products

    def fold(g):
        n = g.shape[0] // 2
        g = g[0:n] + g[n:2 * n]
        return g + pltpu.roll(g, 64, 1)

    def pack(g):
        n = g.shape[0] // 2
        mask = lax.broadcasted_iota(jnp.int32, (n, 128), 1) < 64
        return jnp.where(mask, g[0:n], g[n:2 * n])

    def unpack(g):
        n = g.shape[0]
        mask = lax.broadcasted_iota(jnp.int32, (n, 128), 1) < 64
        r = pltpu.roll(g, 64, 1)
        return jnp.concatenate([jnp.where(mask, g, r), jnp.where(mask, r, g)], axis=0)

    spans = []
    base = 0
    for phase in phases:
        spans.append((base, len(phase)))
        base += len(phase)

    def sum_copies(r, f):
        out, inn = (early_out, early_in) if r == 0 else (late_out, late_in)
        base, n = spans[f]
        return [to_remote(out.at[f], inn.at[base + o], red_send.at[r, base + o],
                          red_recv.at[r, base + o], peer(d)) for o, d in enumerate(phases[f])]

    def sum_start(r, f, value):
        (early_out if r == 0 else late_out)[f] = value
        for copy in sum_copies(r, f):
            copy.start()

    def sum_finish(r, f, value):
        inn = early_in if r == 0 else late_in
        base, n = spans[f]
        for copy in sum_copies(r, f):
            copy.wait_recv()
        parts = [value] + [inn[base + o] for o in range(n)]
        while len(parts) > 1:
            parts = [parts[i] + parts[i + 1] if i + 1 < len(parts) else parts[i]
                     for i in range(0, len(parts), 2)]
        return parts[0]

    lax.fori_loop(0, S - 1, step, 0)
    halves[:, :, S - 1] = jnp.zeros((PAIRS, 2, NRHS, 128), BF16)
    gram = products(slice(0, 3), slice(0, 4), 0, PAIRS)
    early = pack(fold(gram))
    sum_start(0, 0, early)
    apply_pairs(S - 1, range(EDGE, PAIRS - EDGE), -2.0)
    new, every = slice(3, 4), slice(0, 4)
    inside = products(new, every, EDGE, PAIRS - 2 * EDGE)
    edges(S - 1, -2.0, 1.0, None, True)
    late = pack(fold(inside + products(new, every, 0, EDGE)
                     + products(new, every, PAIRS - EDGE, EDGE)))
    sum_start(1, 0, late)
    early = sum_finish(0, 0, early)
    sum_start(0, 1, early)
    late = sum_finish(1, 0, late)
    sum_start(1, 1, late)
    early = sum_finish(0, 1, early)

    gram = unpack(early)
    lane32 = lax.broadcasted_iota(jnp.int32, (32, 128), 1)
    sub32 = lax.broadcasted_iota(jnp.int32, (32, 128), 0)
    hess = gram[16:48] + 2.0 * gram[0:32]
    system = pltpu.roll(hess, 112, 1) + jnp.where(lane32 % 64 < 48, 2.0 * hess, 0.0)
    system = jnp.where(lane32 < 64, system, jnp.where(lane32 - 64 == sub32, 1.0, 0.0))
    system = eliminate(system, 0, 32)

    late = unpack(sum_finish(1, 1, late))
    lane16 = lax.broadcasted_iota(jnp.int32, (16, 128), 1)
    turned = jnp.transpose(jnp.concatenate([late, jnp.zeros((112, 128), F32)], axis=0))
    row2 = jnp.where(lane16 % 64 < 48, gram[32:48],
                     pltpu.roll(turned[32:48], 48, 1))
    hess2 = late + 2.0 * row2
    cross = pltpu.roll(hess2, 112, 1) + jnp.where(lane16 % 64 < 48, 2.0 * hess2, 0.0)
    hp = lax.Precision.HIGHEST
    moved = jnp.dot(cross[:, 0:32], system, precision=hp, preferred_element_type=F32)
    inner = lax.dot_general(moved[:, 64:96], cross[:, 0:32], (((1,), (1,)), ((), ())),
                            precision=hp, preferred_element_type=F32)
    inner = jnp.concatenate([inner, jnp.zeros((16, 112), F32)], axis=1)
    schur = jnp.where(lane16 < 16, pltpu.roll(cross, 96, 1) - inner,
                      pltpu.roll(cross - moved, 96, 1))
    schur = eliminate(schur, 0, 16)
    last = pltpu.roll(schur, 32, 1)
    back = jnp.transpose(jnp.concatenate([moved, jnp.zeros((112, 128), F32)], axis=0))[64:96, 0:16]
    first = system - jnp.dot(back, last, precision=hp, preferred_element_type=F32)
    system = jnp.concatenate([first, last], axis=0)

    none = jnp.zeros((16, 128), F32)
    low_coeff = jnp.concatenate([system, none], axis=0)
    high_coeff = jnp.concatenate([none, system], axis=0) + 2.0 * low_coeff
    lane = lax.broadcasted_iota(jnp.int32, (64, 128), 1)
    mix = jnp.where(lane < 16, pltpu.roll(low_coeff, 80, 1), pltpu.roll(-high_coeff, 96, 1))
    mix = jnp.transpose(mix)[0:32]

    outs = []
    for p in range(0, PAIRS, 4):
        tile = jnp.concatenate([basis[:, p + t].reshape(64, 128) for t in range(4)], axis=1)
        out = jnp.dot(mix, tile, precision=lax.Precision.HIGHEST, preferred_element_type=F32)
        lanes = slice(p * 128, (p + 4) * 128)
        guess[:, lanes] = x_ref[:, lanes] + out[0:16]
        guess[:, slice(p * 128 + 2048, p * 128 + 2560)] = tile[0:16] + out[16:32]
        for w in range(2):
            src, dst = guess, guess_hbm
            lanes = slice(p * 128 + w * 2048, p * 128 + w * 2048 + 512)
            copy = pltpu.make_async_copy(src.at[:, lanes], dst.at[:, lanes],
                                         out_sem.at[w, p // 4])
            copy.start()
            outs.append(copy)

    for w in range(2):
        for q in range(EDGE):
            first_halo(w, q).wait_send()
        for j in range(1, S):
            later_halo(j, w).wait_send()
    for r in range(2):
        for f in range(2):
            for copy in sum_copies(r, f):
                copy.wait_send()
    for copy in outs:
        copy.wait()


def per_device(sizes, blocks, col_index, right_side, start_guess):
    n_red = sum(len(z) * len(y) * len(x) * len(c) - 1 for z, y, x, c in PHASES(sizes))
    anywhere = pl.BlockSpec(memory_space=pltpu.HBM)
    dma = pltpu.SemaphoreType.DMA
    out = jax.ShapeDtypeStruct((NRHS, ROWS * BS), F32)
    out = pl.pallas_call(
        functools.partial(kernel, sizes),
        out_shape=jax.ShapeDtypeStruct((NRHS, 2 * ROWS * BS), F32),
        in_specs=[pl.BlockSpec(memory_space=pltpu.SMEM), anywhere, anywhere, anywhere],
        out_specs=anywhere,
        scratch_shapes=[
            pltpu.SMEM((NNZB, ROWS), jnp.int32),
            pltpu.VMEM((ROWS, NNZB, BS, BS), F32),
            pltpu.VMEM((ROWS, 2 * BS, NNZB * BS), BF16),
            pltpu.VMEM((NRHS, ROWS * BS), F32),
            pltpu.VMEM((NRHS, ROWS * BS), F32),
            pltpu.VMEM((S + 1, ROWS + 2 * BAND, 2 * NRHS, 128), BF16),
            pltpu.VMEM((ROWS, NRHS, 128), F32),
            pltpu.VMEM((S, PAIRS, NRHS, 128), F32),
            pltpu.VMEM((PAIRS, 2, S, NRHS, 128), BF16),
            pltpu.VMEM((S, 2, EDGE, NRHS, 128), F32),
            pltpu.VMEM((2, 24, 128), F32),
            pltpu.VMEM((n_red, 24, 128), F32),
            pltpu.VMEM((2, 8, 128), F32),
            pltpu.VMEM((n_red, 8, 128), F32),
            pltpu.VMEM((NRHS, 2 * ROWS * BS), F32),
            dma((ROWS // CHUNK,)),
            dma((2,)),
            dma((2, EDGE)),
            dma((2, EDGE)),
            dma((S - 1, 2)),
            dma((S - 1, 2)),
            dma((2, n_red)),
            dma((2, n_red)),
            dma((2, PAIRS // 4)),
        ],
        compiler_params=pltpu.CompilerParams(
            collective_id=0, has_side_effects=True, vmem_limit_bytes=62 * 1024 * 1024),
        name="gmres_cycle",
    )(col_index.T, blocks, right_side, start_guess)
    return out[:, :ROWS * BS], out[:, ROWS * BS:]


def solution(mesh, sizes=(8, 4, 4, 2)):
    torus = Mesh(mesh.devices.reshape(sizes), AXES)
    in_specs = (P(AXES, None, None, None), P(AXES, None), P(None, AXES), P(None, AXES))
    out_specs = (P(None, AXES), P(None, AXES))
    return jax.shard_map(functools.partial(per_device, sizes), mesh=torus, in_specs=in_specs,
                         out_specs=out_specs, check_vma=False)
```

```python
import functools
import itertools

import jax
import jax.numpy as jnp
from jax import lax
from jax.experimental import pallas as pl
from jax.experimental.pallas import tpu as pltpu
from jax.sharding import Mesh
from jax.sharding import PartitionSpec as P

BS = 64
STEPS = 4
NNZB = 8
NRHS = 16
S = 4
BAND = 8
ROWS = 32
PAIRS = ROWS // 2
EDGE = BAND // 2
CHUNK = 4
AXES = ("z", "y", "x", "c")
F32 = jnp.float32
BF16 = jnp.bfloat16


def PHASES(sizes):
    nz, ny, nx, nc = sizes
    one = range(1)
    return ((one, range(ny), range(nx), range(nc)), (range(nz), one, one, one))


def split(v):
    high = v.astype(BF16)
    low = (v - high.astype(F32)).astype(BF16)
    return high, low


def dot_nt(a, b):
    return lax.dot_general(a, b, (((1,), (1,)), ((), ())), preferred_element_type=F32)


def eliminate(system, start, n):
    rows = system.shape[0]
    sub = lax.broadcasted_iota(jnp.int32, system.shape, 0)
    for k in range(start, start + n, STEPS):
        cols = [jnp.broadcast_to(system[:, k + i:k + i + 1], system.shape) for i in range(STEPS)]
        rows = []
        for i in range(STEPS):
            row = system[k + i:k + i + 1]
            lead = [cols[m][k + i:k + i + 1] for m in range(STEPS)]
            rows.append((row, lead))
        done = [r for r, _ in rows]
        lead = [l for _, l in rows]
        for i in range(STEPS):
            inv = 1.0 / lead[i][i]
            done[i] = done[i] * inv
            lead[i] = [v * inv for v in lead[i]]
            for m in range(STEPS):
                if m != i:
                    factor = lead[m][i]
                    done[m] = done[m] - factor * done[i]
                    lead[m] = [a - factor * b for a, b in zip(lead[m], lead[i])]
        block = system
        for i in range(STEPS):
            block = block - cols[i] * done[i]
        for i in range(STEPS):
            block = jnp.where(sub == k + i, done[i], block)
        system = block
    return system


def kernel(sizes, col_ref, blocks_hbm, b_hbm, x_hbm, guess_hbm,
           at_ref, raw, mat, b_ref, x_ref, vec, dup, basis, halves, halo, early_out, early_in, late_out, late_in,
           guess, raw_sem, in_sem, halo0_send, halo0_recv, halo_send, halo_recv,
           red_send, red_recv, out_sem):
    nz, ny, nx, nc = sizes
    total = nz * ny * nx * nc
    here = tuple(lax.axis_index(a) for a in AXES)
    z, y, x, c = here
    linear = ((z * ny + y) * nx + x) * nc + c

    def place(d):
        return (d // (ny * nx * nc), (d // (nx * nc)) % ny, (d // nc) % nx, d % nc)

    up = place((linear + 1) % total)
    down = place((linear + total - 1) % total)

    def offsets(zs, ys, xs, cs):
        def hops(d):
            return sum(min(v, n - v) for v, n in zip(d[:3], (nz, ny, nx)))
        found = [d for d in itertools.product(zs, ys, xs, cs) if any(d)]
        return sorted(found, key=lambda d: (-hops(d), d))

    def peer(d):
        return tuple((v + o) % n for v, o, n in zip(here, d, sizes))

    phases = tuple(offsets(*span) for span in PHASES(sizes))
    order = jnp.where(linear % (nx * nc) == nx * nc - 1, 1, 0)

    def to_remote(src, dst, send, recv, dev):
        return pltpu.make_async_remote_copy(
            src_ref=src, dst_ref=dst, send_sem=send, recv_sem=recv,
            device_id=dev, device_id_type=pl.DeviceIdType.MESH)

    barrier = pltpu.get_barrier_semaphore()
    count = 2
    for dev in (up, down):
        pl.semaphore_signal(barrier, inc=1, device_id=dev, device_id_type=pl.DeviceIdType.MESH)
    for d in sorted(phases[0] + phases[1], key=lambda d: -sum(min(v, n - v) for v, n in zip(d, sizes))):
        count += 1
        pl.semaphore_signal(barrier, inc=1, device_id=peer(d),
                            device_id_type=pl.DeviceIdType.MESH)

    load_x = pltpu.make_async_copy(x_hbm, x_ref, in_sem.at[0])
    load_b = pltpu.make_async_copy(b_hbm, b_ref, in_sem.at[1])
    load_x.start()
    load_b.start()

    def load_blocks(n):
        rows = pl.ds(n * CHUNK, CHUNK)
        return pltpu.make_async_copy(blocks_hbm.at[rows], raw.at[rows], raw_sem.at[n])

    for n in range(ROWS // CHUNK):
        load_blocks(n).start()
    first_row = linear * ROWS

    def locate(g, _):
        for k in range(NNZB):
            at = jnp.bitwise_and(col_ref[k, g] - first_row + BAND + total * ROWS,
                                 total * ROWS - 1)
            at_ref[k, g] = jnp.minimum(at, ROWS + 2 * BAND - 1)
        return 0

    lax.fori_loop(0, ROWS, locate, 0)
    pl.semaphore_wait(barrier, count)

    def neighbour(w):
        return tuple(jnp.where(w == 1, u, d) for u, d in zip(up, down))

    def first_halo(w, q):
        tile = q + w * (PAIRS - EDGE)
        return to_remote(x_hbm.at[:, pl.ds(pl.multiple_of(tile * 128, 128), 128)],
                         halo.at[0, 1 - w, q], halo0_send.at[w, q], halo0_recv.at[1 - w, q],
                         neighbour(w))

    def later_halo(j, w):
        return to_remote(basis.at[j - 1, pl.ds(w * (PAIRS - EDGE), EDGE)], halo.at[j, 1 - w],
                         halo_send.at[j - 1, w], halo_recv.at[j - 1, 1 - w], neighbour(w))

    for w in (order, 1 - order):
        for q in range(EDGE):
            first_halo(w, q).start()

    left = lax.broadcasted_iota(jnp.int32, (NRHS, 128), 1) < BS
    left2 = lax.broadcasted_iota(jnp.int32, (2 * NRHS, 128), 1) < BS

    def both(v):
        r = pltpu.roll(v, BS, 1)
        return jnp.where(left, v, r), jnp.where(left, r, v)

    def put(j, row, v):
        high, low = split(v)
        vec[j, row, 0:NRHS] = high
        vec[j, row, NRHS:2 * NRHS] = low

    load_x.wait()
    load_b.wait()

    def spread(p, _):
        lanes = pl.ds(pl.multiple_of(p * 128, 128), 128)
        v0, v1 = both(-x_ref[:, lanes])
        put(0, BAND + 2 * p, v0)
        put(0, BAND + 2 * p + 1, v1)
        w0, w1 = both(b_ref[:, lanes])
        dup[2 * p] = w0
        dup[2 * p + 1] = w1
        return 0

    lax.fori_loop(0, PAIRS, spread, 0)

    def prepare_row(g):
        for m in range(NNZB // 2):
            wide = jnp.concatenate([raw[g, 2 * m], raw[g, 2 * m + 1]], axis=1)
            high, low = split(wide)
            mat[g, 0:BS, m * 128:(m + 1) * 128] = high
            mat[g, BS:2 * BS, m * 128:(m + 1) * 128] = low

    def prepare(n, _):
        load_blocks(n).wait()
        for r in range(CHUNK):
            prepare_row(n * CHUNK + r)
        return 0

    lax.fori_loop(0, ROWS // CHUNK, prepare, 0)

    def apply_pairs(j, pairs, beta):
        halfs = []
        for p in pairs:
            for g in (2 * p, 2 * p + 1):
                tiles = []
                for m in range(NNZB // 2):
                    tiles.append(jnp.where(left2, vec[j, at_ref[2 * m, g]],
                                           vec[j, at_ref[2 * m + 1, g]]))
                out = dot_nt(jnp.concatenate(tiles, axis=1), mat[g])
                halfs.append(out[0:NRHS] + out[NRHS:2 * NRHS])
        for i, p in enumerate(pairs):
            v = []
            for g in (0, 1):
                half = halfs[2 * i + g]
                v.append(half + pltpu.roll(half, BS, 1) + beta * dup[2 * p + g])
            for g in (0, 1):
                dup[2 * p + g] = v[g]
                put(j + 1, BAND + 2 * p + g, v[g])
            both_rows = jnp.where(left, v[0], v[1])
            basis[j, p] = both_rows
            high, low = split(both_rows)
            halves[p, 0, j] = high
            halves[p, 1, j] = low

    def take_halo(j, w, sign):
        for q in range(EDGE):
            v0, v1 = both(sign * halo[j, w, q])
            row = 2 * q + w * (BAND + ROWS)
            put(j, row, v0)
            put(j, row + 1, v1)

    def edges(j, beta, sign, first, last):
        for w in (order, 1 - order):
            if first is None:
                later_halo(j, 1 - w).wait_recv()
            else:
                @pl.when(first)
                def _():
                    for q in range(EDGE):
                        first_halo(1 - w, q).wait_recv()

                @pl.when(jnp.logical_not(first))
                def _():
                    later_halo(j, 1 - w).wait_recv()

            take_halo(j, w, sign)
            start = w * (PAIRS - EDGE)
            apply_pairs(j, [start + i for i in range(EDGE)], beta)
            if not last:
                later_halo(j + 1, w).start()

    def step(j, _):
        beta = jnp.where(j == 0, 1.0, -2.0)
        sign = jnp.where(j == 0, -1.0, 1.0)
        apply_pairs(j, range(EDGE, PAIRS - EDGE), beta)
        edges(j, beta, sign, j == 0, False)
        return 0

    def products(rows, cols, start, n):
        total_products = None
        for p in range(start, start + n, 2):
            def tile(js):
                return jnp.concatenate(
                    [halves[q][:, js].reshape(2 * len(range(S)[js]) * NRHS, 128)
                     for q in (p, p + 1)], axis=1)
            part = dot_nt(tile(rows), tile(cols))
            total_products = part if total_products is None else total_products + part
        return total_products

    def fold(g):
        n = g.shape[0] // 2
        g = g[0:n] + g[n:2 * n]
        return g + pltpu.roll(g, 64, 1)

    def pack(g):
        n = g.shape[0] // 2
        mask = lax.broadcasted_iota(jnp.int32, (n, 128), 1) < 64
        return jnp.where(mask, g[0:n], g[n:2 * n])

    def unpack(g):
        n = g.shape[0]
        mask = lax.broadcasted_iota(jnp.int32, (n, 128), 1) < 64
        r = pltpu.roll(g, 64, 1)
        return jnp.concatenate([jnp.where(mask, g, r), jnp.where(mask, r, g)], axis=0)

    spans = []
    base = 0
    for phase in phases:
        spans.append((base, len(phase)))
        base += len(phase)

    def sum_copies(r, f):
        out, inn = (early_out, early_in) if r == 0 else (late_out, late_in)
        base, n = spans[f]
        return [to_remote(out.at[f], inn.at[base + o], red_send.at[r, base + o],
                          red_recv.at[r, base + o], peer(d)) for o, d in enumerate(phases[f])]

    def sum_start(r, f, value):
        (early_out if r == 0 else late_out)[f] = value
        for copy in sum_copies(r, f):
            copy.start()

    def sum_finish(r, f, value):
        inn = early_in if r == 0 else late_in
        base, n = spans[f]
        copies = sum_copies(r, f)
        for o in reversed(range(n)):
            copies[o].wait_recv()
            value = value + inn[base + o]
        return value

    lax.fori_loop(0, S - 1, step, 0)
    halves[:, :, S - 1] = jnp.zeros((PAIRS, 2, NRHS, 128), BF16)
    gram = products(slice(0, 3), slice(0, 4), 0, PAIRS)
    early = pack(fold(gram))
    sum_start(0, 0, early)
    apply_pairs(S - 1, range(EDGE, PAIRS - EDGE), -2.0)
    new, every = slice(3, 4), slice(0, 4)
    inside = products(new, every, EDGE, PAIRS - 2 * EDGE)
    edges(S - 1, -2.0, 1.0, None, True)
    late = pack(fold(inside + products(new, every, 0, EDGE)
                     + products(new, every, PAIRS - EDGE, EDGE)))
    sum_start(1, 0, late)
    early = sum_finish(0, 0, early)
    sum_start(0, 1, early)
    late = sum_finish(1, 0, late)
    sum_start(1, 1, late)
    early = sum_finish(0, 1, early)

    gram = unpack(early)
    lane32 = lax.broadcasted_iota(jnp.int32, (32, 128), 1)
    sub32 = lax.broadcasted_iota(jnp.int32, (32, 128), 0)
    hess = gram[16:48] + 2.0 * gram[0:32]
    system = pltpu.roll(hess, 112, 1) + jnp.where(lane32 % 64 < 48, 2.0 * hess, 0.0)
    system = jnp.where(lane32 < 64, system, jnp.where(lane32 - 64 == sub32, 1.0, 0.0))
    system = eliminate(system, 0, 32)

    for w in range(2):
        for q in range(EDGE):
            first_halo(w, q).wait_send()
        for j in range(1, S):
            later_halo(j, w).wait_send()
    for copy in sum_copies(0, 0) + sum_copies(0, 1) + sum_copies(1, 0):
        copy.wait_send()
    late = unpack(sum_finish(1, 1, late))
    lane16 = lax.broadcasted_iota(jnp.int32, (16, 128), 1)
    turned = jnp.transpose(jnp.concatenate([late, jnp.zeros((112, 128), F32)], axis=0))
    row2 = jnp.where(lane16 % 64 < 48, gram[32:48],
                     pltpu.roll(turned[32:48], 48, 1))
    hess2 = late + 2.0 * row2
    cross = pltpu.roll(hess2, 112, 1) + jnp.where(lane16 % 64 < 48, 2.0 * hess2, 0.0)
    hp = lax.Precision.HIGHEST
    moved = jnp.dot(cross[:, 0:32], system, precision=hp, preferred_element_type=F32)
    inner = lax.dot_general(moved[:, 64:96], cross[:, 0:32], (((1,), (1,)), ((), ())),
                            precision=hp, preferred_element_type=F32)
    inner = jnp.concatenate([inner, jnp.zeros((16, 112), F32)], axis=1)
    schur = jnp.where(lane16 < 16, pltpu.roll(cross, 96, 1) - inner,
                      pltpu.roll(cross - moved, 96, 1))
    schur = eliminate(schur, 0, 16)
    last = pltpu.roll(schur, 32, 1)
    back = jnp.transpose(jnp.concatenate([moved, jnp.zeros((112, 128), F32)], axis=0))[64:96, 0:16]
    first = system - jnp.dot(back, last, precision=hp, preferred_element_type=F32)
    system = jnp.concatenate([first, last], axis=0)

    none = jnp.zeros((16, 128), F32)
    low_coeff = jnp.concatenate([system, none], axis=0)
    high_coeff = jnp.concatenate([none, system], axis=0) + 2.0 * low_coeff
    lane = lax.broadcasted_iota(jnp.int32, (64, 128), 1)
    mix = jnp.where(lane < 16, pltpu.roll(low_coeff, 80, 1), pltpu.roll(-high_coeff, 96, 1))
    mix = jnp.transpose(mix)[0:32]

    outs = []
    for p in range(0, PAIRS, 4):
        tile = jnp.concatenate([basis[:, p + t].reshape(64, 128) for t in range(4)], axis=1)
        out = jnp.dot(mix, tile, precision=lax.Precision.HIGHEST, preferred_element_type=F32)
        lanes = slice(p * 128, (p + 4) * 128)
        guess[:, lanes] = x_ref[:, lanes] + out[0:16]
        guess[:, slice(p * 128 + 2048, p * 128 + 2560)] = tile[0:16] + out[16:32]
        for w in range(2):
            src, dst = guess, guess_hbm
            lanes = slice(p * 128 + w * 2048, p * 128 + w * 2048 + 512)
            copy = pltpu.make_async_copy(src.at[:, lanes], dst.at[:, lanes],
                                         out_sem.at[w, p // 4])
            copy.start()
            outs.append(copy)

    for copy in sum_copies(1, 1):
        copy.wait_send()
    for copy in outs:
        copy.wait()


def per_device(sizes, blocks, col_index, right_side, start_guess):
    n_red = sum(len(z) * len(y) * len(x) * len(c) - 1 for z, y, x, c in PHASES(sizes))
    anywhere = pl.BlockSpec(memory_space=pltpu.HBM)
    dma = pltpu.SemaphoreType.DMA
    out = jax.ShapeDtypeStruct((NRHS, ROWS * BS), F32)
    out = pl.pallas_call(
        functools.partial(kernel, sizes),
        out_shape=jax.ShapeDtypeStruct((NRHS, 2 * ROWS * BS), F32),
        in_specs=[pl.BlockSpec(memory_space=pltpu.SMEM), anywhere, anywhere, anywhere],
        out_specs=anywhere,
        scratch_shapes=[
            pltpu.SMEM((NNZB, ROWS), jnp.int32),
            pltpu.VMEM((ROWS, NNZB, BS, BS), F32),
            pltpu.VMEM((ROWS, 2 * BS, NNZB * BS), BF16),
            pltpu.VMEM((NRHS, ROWS * BS), F32),
            pltpu.VMEM((NRHS, ROWS * BS), F32),
            pltpu.VMEM((S + 1, ROWS + 2 * BAND, 2 * NRHS, 128), BF16),
            pltpu.VMEM((ROWS, NRHS, 128), F32),
            pltpu.VMEM((S, PAIRS, NRHS, 128), F32),
            pltpu.VMEM((PAIRS, 2, S, NRHS, 128), BF16),
            pltpu.VMEM((S, 2, EDGE, NRHS, 128), F32),
            pltpu.VMEM((2, 24, 128), F32),
            pltpu.VMEM((n_red, 24, 128), F32),
            pltpu.VMEM((2, 8, 128), F32),
            pltpu.VMEM((n_red, 8, 128), F32),
            pltpu.VMEM((NRHS, 2 * ROWS * BS), F32),
            dma((ROWS // CHUNK,)),
            dma((2,)),
            dma((2, EDGE)),
            dma((2, EDGE)),
            dma((S - 1, 2)),
            dma((S - 1, 2)),
            dma((2, n_red)),
            dma((2, n_red)),
            dma((2, PAIRS // 4)),
        ],
        compiler_params=pltpu.CompilerParams(
            collective_id=0, has_side_effects=True, vmem_limit_bytes=62 * 1024 * 1024),
        name="gmres_cycle",
    )(col_index.T, blocks, right_side, start_guess)
    return out[:, :ROWS * BS], out[:, ROWS * BS:]


def solution(mesh, sizes=(8, 4, 4, 2)):
    torus = Mesh(mesh.devices.reshape(sizes), AXES)
    in_specs = (P(AXES, None, None, None), P(AXES, None), P(None, AXES), P(None, AXES))
    out_specs = (P(None, AXES), P(None, AXES))
    return jax.shard_map(functools.partial(per_device, sizes), mesh=torus, in_specs=in_specs,
                         out_specs=out_specs, check_vma=False)
```

```python
import functools
import itertools

import jax
import jax.numpy as jnp
from jax import lax
from jax.experimental import pallas as pl
from jax.experimental.pallas import tpu as pltpu
from jax.sharding import Mesh
from jax.sharding import PartitionSpec as P

BS = 64
STEPS = 4
NNZB = 8
NRHS = 16
S = 4
BAND = 8
ROWS = 32
PAIRS = ROWS // 2
EDGE = BAND // 2
CHUNK = 4
AXES = ("z", "y", "x", "c")
F32 = jnp.float32
BF16 = jnp.bfloat16


def PHASES(sizes):
    nz, ny, nx, nc = sizes
    one = range(1)
    return ((one, range(ny), range(nx), range(nc)), (range(nz), one, one, one))


def split(v):
    high = v.astype(BF16)
    low = (v - high.astype(F32)).astype(BF16)
    return high, low


def dot_nt(a, b):
    return lax.dot_general(a, b, (((1,), (1,)), ((), ())), preferred_element_type=F32)


def eliminate(system, start, n):
    rows = system.shape[0]
    sub = lax.broadcasted_iota(jnp.int32, system.shape, 0)
    for k in range(start, start + n, STEPS):
        cols = [jnp.broadcast_to(system[:, k + i:k + i + 1], system.shape) for i in range(STEPS)]
        rows = []
        for i in range(STEPS):
            row = system[k + i:k + i + 1]
            lead = [cols[m][k + i:k + i + 1] for m in range(STEPS)]
            rows.append((row, lead))
        done = [r for r, _ in rows]
        lead = [l for _, l in rows]
        for i in range(STEPS):
            inv = 1.0 / lead[i][i]
            done[i] = done[i] * inv
            lead[i] = [v * inv for v in lead[i]]
            for m in range(STEPS):
                if m != i:
                    factor = lead[m][i]
                    done[m] = done[m] - factor * done[i]
                    lead[m] = [a - factor * b for a, b in zip(lead[m], lead[i])]
        block = system
        for i in range(STEPS):
            block = block - cols[i] * done[i]
        for i in range(STEPS):
            block = jnp.where(sub == k + i, done[i], block)
        system = block
    return system


def kernel(sizes, col_ref, blocks_hbm, b_hbm, x_hbm, guess_hbm,
           at_ref, raw, mat, b_ref, x_ref, vec, dup, basis, halves, halo, early_out, early_in, late_out, late_in,
           guess, raw_sem, in_sem, halo0_send, halo0_recv, halo_send, halo_recv,
           red_send, red_recv, out_sem):
    nz, ny, nx, nc = sizes
    total = nz * ny * nx * nc
    here = tuple(lax.axis_index(a) for a in AXES)
    z, y, x, c = here
    linear = ((z * ny + y) * nx + x) * nc + c

    def place(d):
        return (d // (ny * nx * nc), (d // (nx * nc)) % ny, (d // nc) % nx, d % nc)

    up = place((linear + 1) % total)
    down = place((linear + total - 1) % total)

    def offsets(zs, ys, xs, cs):
        def hops(d):
            return sum(min(v, n - v) for v, n in zip(d[:3], (nz, ny, nx)))
        found = [d for d in itertools.product(zs, ys, xs, cs) if any(d)]
        return sorted(found, key=lambda d: (-hops(d), d))

    def peer(d):
        return tuple((v + o) % n for v, o, n in zip(here, d, sizes))

    phases = tuple(offsets(*span) for span in PHASES(sizes))
    order = jnp.where(linear % (nx * nc) == nx * nc - 1, 1, 0)

    def to_remote(src, dst, send, recv, dev):
        return pltpu.make_async_remote_copy(
            src_ref=src, dst_ref=dst, send_sem=send, recv_sem=recv,
            device_id=dev, device_id_type=pl.DeviceIdType.MESH)

    barrier = pltpu.get_barrier_semaphore()
    count = 2
    for dev in (up, down):
        pl.semaphore_signal(barrier, inc=1, device_id=dev, device_id_type=pl.DeviceIdType.MESH)
    for d in sorted(phases[0] + phases[1], key=lambda d: -sum(min(v, n - v) for v, n in zip(d, sizes))):
        count += 1
        pl.semaphore_signal(barrier, inc=1, device_id=peer(d),
                            device_id_type=pl.DeviceIdType.MESH)

    load_x = pltpu.make_async_copy(x_hbm, x_ref, in_sem.at[0])
    load_b = pltpu.make_async_copy(b_hbm, b_ref, in_sem.at[1])
    load_x.start()
    load_b.start()

    def load_blocks(n):
        rows = pl.ds(n * CHUNK, CHUNK)
        return pltpu.make_async_copy(blocks_hbm.at[rows], raw.at[rows], raw_sem.at[n])

    for n in range(ROWS // CHUNK):
        load_blocks(n).start()
    first_row = linear * ROWS

    def locate(g, _):
        for k in range(NNZB):
            at = jnp.bitwise_and(col_ref[k, g] - first_row + BAND + total * ROWS,
                                 total * ROWS - 1)
            at_ref[k, g] = jnp.minimum(at, ROWS + 2 * BAND - 1)
        return 0

    lax.fori_loop(0, ROWS, locate, 0)
    pl.semaphore_wait(barrier, count)

    def neighbour(w):
        return tuple(jnp.where(w == 1, u, d) for u, d in zip(up, down))

    def first_halo(w, q):
        tile = q + w * (PAIRS - EDGE)
        return to_remote(x_hbm.at[:, pl.ds(pl.multiple_of(tile * 128, 128), 128)],
                         halo.at[0, 1 - w, q], halo0_send.at[w, q], halo0_recv.at[1 - w, q],
                         neighbour(w))

    def later_halo(j, w):
        return to_remote(basis.at[j - 1, pl.ds(w * (PAIRS - EDGE), EDGE)], halo.at[j, 1 - w],
                         halo_send.at[j - 1, w], halo_recv.at[j - 1, 1 - w], neighbour(w))

    for w in (order, 1 - order):
        for q in range(EDGE):
            first_halo(w, q).start()

    left = lax.broadcasted_iota(jnp.int32, (NRHS, 128), 1) < BS
    left2 = lax.broadcasted_iota(jnp.int32, (2 * NRHS, 128), 1) < BS

    def both(v):
        r = pltpu.roll(v, BS, 1)
        return jnp.where(left, v, r), jnp.where(left, r, v)

    def put(j, row, v):
        high, low = split(v)
        vec[j, row, 0:NRHS] = high
        vec[j, row, NRHS:2 * NRHS] = low

    load_x.wait()
    load_b.wait()

    def spread(p, _):
        lanes = pl.ds(pl.multiple_of(p * 128, 128), 128)
        v0, v1 = both(-x_ref[:, lanes])
        put(0, BAND + 2 * p, v0)
        put(0, BAND + 2 * p + 1, v1)
        w0, w1 = both(b_ref[:, lanes])
        dup[2 * p] = w0
        dup[2 * p + 1] = w1
        return 0

    lax.fori_loop(0, PAIRS, spread, 0)

    def prepare_row(g):
        for m in range(NNZB // 2):
            wide = jnp.concatenate([raw[g, 2 * m], raw[g, 2 * m + 1]], axis=1)
            high, low = split(wide)
            mat[g, 0:BS, m * 128:(m + 1) * 128] = high
            mat[g, BS:2 * BS, m * 128:(m + 1) * 128] = low

    def prepare(n, _):
        load_blocks(n).wait()
        for r in range(CHUNK):
            prepare_row(n * CHUNK + r)
        return 0

    lax.fori_loop(0, ROWS // CHUNK, prepare, 0)

    def apply_pairs(j, pairs, beta):
        halfs = []
        for p in pairs:
            for g in (2 * p, 2 * p + 1):
                tiles = []
                for m in range(NNZB // 2):
                    tiles.append(jnp.where(left2, vec[j, at_ref[2 * m, g]],
                                           vec[j, at_ref[2 * m + 1, g]]))
                out = dot_nt(jnp.concatenate(tiles, axis=1), mat[g])
                halfs.append(out[0:NRHS] + out[NRHS:2 * NRHS])
        for i, p in enumerate(pairs):
            v = []
            for g in (0, 1):
                half = halfs[2 * i + g]
                v.append(half + pltpu.roll(half, BS, 1) + beta * dup[2 * p + g])
            for g in (0, 1):
                dup[2 * p + g] = v[g]
                put(j + 1, BAND + 2 * p + g, v[g])
            both_rows = jnp.where(left, v[0], v[1])
            basis[j, p] = both_rows
            high, low = split(both_rows)
            halves[p, 0, j] = high
            halves[p, 1, j] = low

    def take_halo(j, w, sign):
        for q in range(EDGE):
            v0, v1 = both(sign * halo[j, w, q])
            row = 2 * q + w * (BAND + ROWS)
            put(j, row, v0)
            put(j, row + 1, v1)

    def edges(j, beta, sign, first, last):
        for w in (order, 1 - order):
            if first is None:
                later_halo(j, 1 - w).wait_recv()
            else:
                @pl.when(first)
                def _():
                    for q in range(EDGE):
                        first_halo(1 - w, q).wait_recv()

                @pl.when(jnp.logical_not(first))
                def _():
                    later_halo(j, 1 - w).wait_recv()

            take_halo(j, w, sign)
            start = w * (PAIRS - EDGE)
            apply_pairs(j, [start + i for i in range(EDGE)], beta)
            if not last:
                later_halo(j + 1, w).start()

    def step(j, _):
        beta = jnp.where(j == 0, 1.0, -2.0)
        sign = jnp.where(j == 0, -1.0, 1.0)
        apply_pairs(j, range(EDGE, PAIRS - EDGE), beta)
        edges(j, beta, sign, j == 0, False)
        return 0

    def products(rows, cols, start, n):
        total_products = None
        for p in range(start, start + n, 2):
            def tile(js):
                return jnp.concatenate(
                    [halves[q][:, js].reshape(2 * len(range(S)[js]) * NRHS, 128)
                     for q in (p, p + 1)], axis=1)
            part = dot_nt(tile(rows), tile(cols))
            total_products = part if total_products is None else total_products + part
        return total_products

    def fold(g):
        n = g.shape[0] // 2
        g = g[0:n] + g[n:2 * n]
        return g + pltpu.roll(g, 64, 1)

    def pack(g):
        n = g.shape[0] // 2
        mask = lax.broadcasted_iota(jnp.int32, (n, 128), 1) < 64
        return jnp.where(mask, g[0:n], g[n:2 * n])

    def unpack(g):
        n = g.shape[0]
        mask = lax.broadcasted_iota(jnp.int32, (n, 128), 1) < 64
        r = pltpu.roll(g, 64, 1)
        return jnp.concatenate([jnp.where(mask, g, r), jnp.where(mask, r, g)], axis=0)

    spans = []
    base = 0
    for phase in phases:
        spans.append((base, len(phase)))
        base += len(phase)

    def sum_copies(r, f):
        out, inn = (early_out, early_in) if r == 0 else (late_out, late_in)
        base, n = spans[f]
        return [to_remote(out.at[f], inn.at[base + o], red_send.at[r, base + o],
                          red_recv.at[r, base + o], peer(d)) for o, d in enumerate(phases[f])]

    def sum_start(r, f, value):
        (early_out if r == 0 else late_out)[f] = value
        for copy in sum_copies(r, f):
            copy.start()

    def sum_finish(r, f, value):
        inn = early_in if r == 0 else late_in
        base, n = spans[f]
        copies = sum_copies(r, f)
        for o in reversed(range(n)):
            copies[o].wait_recv()
            value = value + inn[base + o]
        return value

    lax.fori_loop(0, S - 1, step, 0)
    halves[:, :, S - 1] = jnp.zeros((PAIRS, 2, NRHS, 128), BF16)
    gram = products(slice(0, 3), slice(0, 4), 0, PAIRS)
    early = pack(fold(gram))
    apply_pairs(S - 1, range(EDGE, PAIRS - EDGE), -2.0)
    new, every = slice(3, 4), slice(0, 4)
    inside = products(new, every, EDGE, PAIRS - 2 * EDGE)
    sum_start(0, 0, early)
    edges(S - 1, -2.0, 1.0, None, True)
    late = pack(fold(inside + products(new, every, 0, EDGE)
                     + products(new, every, PAIRS - EDGE, EDGE)))
    sum_start(1, 0, late)
    early = sum_finish(0, 0, early)
    sum_start(0, 1, early)
    late = sum_finish(1, 0, late)
    sum_start(1, 1, late)
    early = sum_finish(0, 1, early)

    gram = unpack(early)
    lane32 = lax.broadcasted_iota(jnp.int32, (32, 128), 1)
    sub32 = lax.broadcasted_iota(jnp.int32, (32, 128), 0)
    hess = gram[16:48] + 2.0 * gram[0:32]
    system = pltpu.roll(hess, 112, 1) + jnp.where(lane32 % 64 < 48, 2.0 * hess, 0.0)
    system = jnp.where(lane32 < 64, system, jnp.where(lane32 - 64 == sub32, 1.0, 0.0))
    system = eliminate(system, 0, 32)

    for w in range(2):
        for q in range(EDGE):
            first_halo(w, q).wait_send()
        for j in range(1, S):
            later_halo(j, w).wait_send()
    for copy in sum_copies(0, 0) + sum_copies(0, 1) + sum_copies(1, 0):
        copy.wait_send()
    late = unpack(sum_finish(1, 1, late))
    lane16 = lax.broadcasted_iota(jnp.int32, (16, 128), 1)
    turned = jnp.transpose(jnp.concatenate([late, jnp.zeros((112, 128), F32)], axis=0))
    row2 = jnp.where(lane16 % 64 < 48, gram[32:48],
                     pltpu.roll(turned[32:48], 48, 1))
    hess2 = late + 2.0 * row2
    cross = pltpu.roll(hess2, 112, 1) + jnp.where(lane16 % 64 < 48, 2.0 * hess2, 0.0)
    hp = lax.Precision.HIGHEST
    moved = jnp.dot(cross[:, 0:32], system, precision=hp, preferred_element_type=F32)
    inner = lax.dot_general(moved[:, 64:96], cross[:, 0:32], (((1,), (1,)), ((), ())),
                            precision=hp, preferred_element_type=F32)
    inner = jnp.concatenate([inner, jnp.zeros((16, 112), F32)], axis=1)
    schur = jnp.where(lane16 < 16, pltpu.roll(cross, 96, 1) - inner,
                      pltpu.roll(cross - moved, 96, 1))
    schur = eliminate(schur, 0, 16)
    last = pltpu.roll(schur, 32, 1)
    back = jnp.transpose(jnp.concatenate([moved, jnp.zeros((112, 128), F32)], axis=0))[64:96, 0:16]
    first = system - jnp.dot(back, last, precision=hp, preferred_element_type=F32)
    system = jnp.concatenate([first, last], axis=0)

    none = jnp.zeros((16, 128), F32)
    low_coeff = jnp.concatenate([system, none], axis=0)
    high_coeff = jnp.concatenate([none, system], axis=0) + 2.0 * low_coeff
    lane = lax.broadcasted_iota(jnp.int32, (64, 128), 1)
    mix = jnp.where(lane < 16, pltpu.roll(low_coeff, 80, 1), pltpu.roll(-high_coeff, 96, 1))
    mix = jnp.transpose(mix)[0:32]

    outs = []
    for p in range(0, PAIRS, 4):
        tile = jnp.concatenate([basis[:, p + t].reshape(64, 128) for t in range(4)], axis=1)
        out = jnp.dot(mix, tile, precision=lax.Precision.HIGHEST, preferred_element_type=F32)
        lanes = slice(p * 128, (p + 4) * 128)
        guess[:, lanes] = x_ref[:, lanes] + out[0:16]
        guess[:, slice(p * 128 + 2048, p * 128 + 2560)] = tile[0:16] + out[16:32]
        for w in range(2):
            src, dst = guess, guess_hbm
            lanes = slice(p * 128 + w * 2048, p * 128 + w * 2048 + 512)
            copy = pltpu.make_async_copy(src.at[:, lanes], dst.at[:, lanes],
                                         out_sem.at[w, p // 4])
            copy.start()
            outs.append(copy)

    for copy in sum_copies(1, 1):
        copy.wait_send()
    for copy in outs:
        copy.wait()


def per_device(sizes, blocks, col_index, right_side, start_guess):
    n_red = sum(len(z) * len(y) * len(x) * len(c) - 1 for z, y, x, c in PHASES(sizes))
    anywhere = pl.BlockSpec(memory_space=pltpu.HBM)
    dma = pltpu.SemaphoreType.DMA
    out = jax.ShapeDtypeStruct((NRHS, ROWS * BS), F32)
    out = pl.pallas_call(
        functools.partial(kernel, sizes),
        out_shape=jax.ShapeDtypeStruct((NRHS, 2 * ROWS * BS), F32),
        in_specs=[pl.BlockSpec(memory_space=pltpu.SMEM), anywhere, anywhere, anywhere],
        out_specs=anywhere,
        scratch_shapes=[
            pltpu.SMEM((NNZB, ROWS), jnp.int32),
            pltpu.VMEM((ROWS, NNZB, BS, BS), F32),
            pltpu.VMEM((ROWS, 2 * BS, NNZB * BS), BF16),
            pltpu.VMEM((NRHS, ROWS * BS), F32),
            pltpu.VMEM((NRHS, ROWS * BS), F32),
            pltpu.VMEM((S + 1, ROWS + 2 * BAND, 2 * NRHS, 128), BF16),
            pltpu.VMEM((ROWS, NRHS, 128), F32),
            pltpu.VMEM((S, PAIRS, NRHS, 128), F32),
            pltpu.VMEM((PAIRS, 2, S, NRHS, 128), BF16),
            pltpu.VMEM((S, 2, EDGE, NRHS, 128), F32),
            pltpu.VMEM((2, 24, 128), F32),
            pltpu.VMEM((n_red, 24, 128), F32),
            pltpu.VMEM((2, 8, 128), F32),
            pltpu.VMEM((n_red, 8, 128), F32),
            pltpu.VMEM((NRHS, 2 * ROWS * BS), F32),
            dma((ROWS // CHUNK,)),
            dma((2,)),
            dma((2, EDGE)),
            dma((2, EDGE)),
            dma((S - 1, 2)),
            dma((S - 1, 2)),
            dma((2, n_red)),
            dma((2, n_red)),
            dma((2, PAIRS // 4)),
        ],
        compiler_params=pltpu.CompilerParams(
            collective_id=0, has_side_effects=True, vmem_limit_bytes=62 * 1024 * 1024),
        name="gmres_cycle",
    )(col_index.T, blocks, right_side, start_guess)
    return out[:, :ROWS * BS], out[:, ROWS * BS:]


def solution(mesh, sizes=(8, 4, 4, 2)):
    torus = Mesh(mesh.devices.reshape(sizes), AXES)
    in_specs = (P(AXES, None, None, None), P(AXES, None), P(None, AXES), P(None, AXES))
    out_specs = (P(None, AXES), P(None, AXES))
    return jax.shard_map(functools.partial(per_device, sizes), mesh=torus, in_specs=in_specs,
                         out_specs=out_specs, check_vma=False)
```
